512 devices in a mesh: gx: 32 (over z, x), gy: 16 (over y, core).
Axes of the slice: x: 4, y: 8, z: 8, core: 2. Of those that a mesh axis runs over, the one named last changes fastest.
Arguments:
- a_blocks: bfloat16 [32, 128, 64, 448], P('gx', 'gy'), may hold values from -0.25 to 0.25
- a_cols: int32 [32, 128, 7], P('gx', 'gy'), may hold values from 0 to 15
- mushy: int32 [32, 128], P('gx', 'gy'), may hold values 0 or 1
- p_blocks: bfloat16 [32, 128, 64, 256], P('gx', 'gy'), may hold values from -0.375 to 0.375
- p_cols: int32 [32, 128, 4], P('gx', 'gy'), may hold values from 0 to 7
- send_rows: int32 [32, 128], P('gx', 'gy'), may hold values from 0 to 7
Outputs:
- coarse_tiles: float32 [32, 512, 1536], P('gx', 'gy')
The draws below stay inside these ranges and needn't reach their ends.
All inputs are finite; a program needn't handle non-finite values. No bound on the sum of `mushy` on one device may be relied on, other than what follows from the above.
Results may differ from the reference program's by a relative error of at most 0.0038.
Values may be sent and summed in bfloat16 or wider, within the bound.
A program may use at most 64 MiB of HBM per device.

```python
import jax
import jax.numpy as jnp
from jax import lax

BS = 64
KA = 7
KS = 3
KP = 4
NCOL = 8
G = 4
NB = 8
ROWS = 128
N_GX = 32
N_GY = 16


def place_ends(entries, rng, least, largest):
    longest = entries.shape.index(max(entries.shape))
    spots = []
    for shift in (0, 1):
        where = [jax.random.randint(jax.random.fold_in(rng, axis), (), 0, length) for axis, length in enumerate(entries.shape)]
        where[longest] = (where[longest] + shift) % entries.shape[longest]
        spots.append(tuple(where))
    return entries.at[spots[0]].set(least).at[spots[1]].set(largest)


def levels(key, extent, cuts, least, top_value):
    factor_of, own = 1.0, jax.random.fold_in(key, 6)
    for axis_at, shards_of in cuts:
        steps = jnp.exp(jax.random.uniform(jax.random.fold_in(own, axis_at), (shards_of,), jnp.float32, least / len(cuts), top_value / len(cuts)))
        factor_of = factor_of * jnp.repeat(steps, extent[axis_at] // shards_of).reshape([-1 if axis == axis_at else 1 for axis in range(len(extent))])
    return factor_of


def bell_draw(own_key, extent, width, most, cuts=(), kind=jnp.bfloat16):
    array = width * jax.random.normal(own_key, extent, jnp.float32)
    if cuts:
        array = array * levels(own_key, extent, cuts, -0.22, 0.18)
    return jnp.clip(array, -most, most).astype(kind)


def setup_inputs(seed: int = 0) -> dict:
    key_of = jax.random.split(jax.random.key(seed), 7)
    return {
        "a_blocks": bell_draw(key_of[0], (N_GX, ROWS, BS, KA * BS), (KA * BS) ** -0.5, 0.25, ((0, 32), (1, 16))),
        "a_cols": place_ends(jax.random.randint(key_of[1], (N_GX, ROWS, KA), 0, NB + 2 * G), jax.random.fold_in(key_of[1], 1), 0, (NB + 2 * G) - 1).astype(jnp.int32),
        "mushy": place_ends((jax.random.randint(key_of[2], (N_GX, ROWS), 0, 3) < 1).astype(jnp.int32), jax.random.fold_in(key_of[2], 1), 0, 1),
        "p_blocks": bell_draw(key_of[3], (N_GX, ROWS, BS, KP * BS), (4 * BS) ** -0.5, 0.375, ((0, 32), (1, 16))),
        "p_cols": place_ends(jax.random.randint(key_of[4], (N_GX, ROWS, KP), 0, NCOL), jax.random.fold_in(key_of[4], 1), 0, NCOL - 1).astype(jnp.int32),
        "send_rows": place_ends(jax.random.randint(key_of[5], (N_GX, N_GY * 2 * G), 0, NB), jax.random.fold_in(key_of[5], 1), 0, NB - 1).astype(jnp.int32),
    }


def dense_rows(blocks, cols, offset, width_blocks):
    count = blocks.shape[0]
    size = blocks.shape[1]
    slots = cols.shape[1]
    onehot = (cols[:, :, None] + offset == jnp.arange(width_blocks, dtype=jnp.int32)[None, None, :]).astype(jnp.float32)
    parts = blocks.reshape(count, size, slots, size).astype(jnp.float32)
    dense = jnp.einsum('rkc,rbka->rbca', onehot, parts)
    return dense.astype(jnp.bfloat16).reshape(count, size, width_blocks * size)


def device_term(ablk, acol, mush, pblk, pcol, left_blk, left_col, right_blk, right_col):
    extended = jnp.concatenate([
        dense_rows(pblk, pcol, NCOL, 3 * NCOL),
        dense_rows(left_blk, left_col, 0, 3 * NCOL),
        dense_rows(right_blk, right_col, 2 * NCOL, 3 * NCOL)], axis=0)
    limit = jnp.where(mush > 0, KA, KS).astype(jnp.int32)
    total = jnp.zeros((NB, BS, 3 * NCOL * BS), jnp.float32)
    for slot in range(KA):
        live = (slot < limit).astype(jnp.bfloat16)
        ablock = ablk[:, :, slot * BS:(slot + 1) * BS] * live[:, None, None]
        picked = extended[acol[:, slot]]
        total = total + jnp.einsum('nij,njw->niw', ablock.astype(jnp.float32), picked.astype(jnp.float32))
    product = total.astype(jnp.bfloat16)
    own = dense_rows(pblk, pcol, 0, NCOL)
    return jnp.einsum('nbc,nbw->cw', own.astype(jnp.float32), product.astype(jnp.float32))


def reference(a_blocks, a_cols, mushy, p_blocks, p_cols, send_rows):
    a4 = a_blocks.reshape(N_GX, N_GY, NB, BS, KA * BS)
    ac4 = a_cols.reshape(N_GX, N_GY, NB, KA)
    m4 = mushy.reshape(N_GX, N_GY, NB)
    p4 = p_blocks.reshape(N_GX, N_GY, NB, BS, KP * BS)
    pc4 = p_cols.reshape(N_GX, N_GY, NB, KP)
    s4 = send_rows.reshape(N_GX, N_GY, 2 * G)

    def column(col):
        left_g = jnp.maximum(col - 1, 0)
        right_g = jnp.minimum(col + 1, N_GX - 1)
        left_flag = (col > 0).astype(jnp.bfloat16)
        right_flag = (col < N_GX - 1).astype(jnp.bfloat16)

        def device(carry, row):
            left_sel = s4[left_g, row, G:]
            right_sel = s4[right_g, row, :G]
            left_blk = p4[left_g, row][left_sel] * left_flag
            left_col = pc4[left_g, row][left_sel]
            right_blk = p4[right_g, row][right_sel] * right_flag
            right_col = pc4[right_g, row][right_sel]
            term = device_term(a4[col, row], ac4[col, row], m4[col, row], p4[col, row], pc4[col, row],
                               left_blk, left_col, right_blk, right_col)
            return carry + term, None

        start = jnp.zeros((NCOL * BS, 3 * NCOL * BS), jnp.float32)
        summed, unused = lax.scan(device, start, jnp.arange(N_GY, dtype=jnp.int32))
        return summed

    return lax.map(column, jnp.arange(N_GX, dtype=jnp.int32))
```

```python
import jax
import jax.numpy as jnp
from jax import lax
from jax.experimental import pallas as pl
from jax.experimental.pallas import tpu as pltpu
from jax.sharding import PartitionSpec as P

KA = 7
KS = 3
KP = 4
NCOL = 8
G = 4
NB = 8
BS = 64
W = NCOL * BS
MESH = pl.DeviceIdType.MESH
LEFT, OWN, RIGHT = 0, 1, 2
GHOST = G * BS


def doubled(tile, low):
    turned = pltpu.roll(tile, BS, 1)
    return jnp.where(low, tile, turned), jnp.where(low, turned, tile)


def kernel(nx, ny, acol, mush, pcol, sends, a_hbm, p_hbm, out_ref,
           a_v, p_v, gsend, grecv, ext, gext, amat, own_t, keep, psend, precv,
           csa, csb, cra, crb,
           load_sem, gs_sem, gr_sem, ps_sem, pr_sem, sa_sem, ra_sem, sb_sem, rb_sem):
    gx = lax.axis_index("gx")
    gy = lax.axis_index("gy")
    yc = gy // 2
    core = gy % 2
    sign = 1 - 2 * core
    west = (gx + nx - 1) % nx
    east = (gx + 1) % nx
    chips = ny // 2

    def chip(by):
        return (yc + sign * by + chips) % chips

    sibling = (gx, yc * 2 + 1 - core)
    ahead = (gx, chip(1) * 2 + core)
    behind = (gx, chip(-1) * 2 + core)

    barrier = pltpu.get_barrier_semaphore()
    for device in ((west, gy), (east, gy), sibling, ahead, behind):
        pl.semaphore_signal(barrier, inc=1, device_id=device, device_id_type=MESH)

    load_p = pltpu.make_async_copy(p_hbm.at[0], p_v, load_sem.at[0])
    load_a = pltpu.make_async_copy(a_hbm.at[0], a_v, load_sem.at[1])
    load_p.start()
    load_a.start()

    def remote(src, dst, send, recv, device):
        return pltpu.make_async_remote_copy(
            src_ref=src, dst_ref=dst, send_sem=send, recv_sem=recv,
            device_id=device, device_id_type=MESH)

    ghosts = [
        remote(gsend.at[side], grecv.at[side], gs_sem.at[side], gr_sem.at[side],
               ((east, west)[side], gy))
        for side in range(2)
    ]
    pairs = [remote(psend.at[part], precv.at[part], ps_sem.at[part], pr_sem.at[part], sibling)
             for part in range(3)]
    chain_a = [[remote(csa.at[part, s], cra.at[part, s], sa_sem.at[part, s], ra_sem.at[part, s], ahead)
                for s in range(4)] for part in range(3)]
    chain_b = [[remote(csb.at[part, s], crb.at[part, s], sb_sem.at[part, s], rb_sem.at[part, s], behind)
                for s in range(3)] for part in range(3)]

    low = lax.broadcasted_iota(jnp.int32, (BS, 2 * BS), 1) < BS
    half = lax.broadcasted_iota(jnp.int32, (1, 2 * BS), 1) // BS
    half_f = half.astype(jnp.float32)

    load_p.wait()
    row_of = lax.broadcasted_iota(jnp.int32, (16, 256), 0)
    for side in range(2):
        codes = jnp.zeros((16, 256), jnp.int32)
        for i in range(G):
            row = sends[0, (1 - side) * G + i]
            gsend[side, i * BS:(i + 1) * BS, :] = p_v[row]
            for j in range(KP):
                codes = jnp.where(row_of == i * KP + j, pcol[0, row, j], codes)
        gsend[side, GHOST:GHOST + 16, :] = codes.astype(jnp.float32).astype(jnp.bfloat16)
    pl.semaphore_wait(barrier, 5)
    for side in range(2):
        ghosts[side].start()

    def placed(block, hits):
        parts = doubled(block[:, :128], low) + doubled(block[:, 128:], low)
        tiles = []
        for q in range(NCOL // 2):
            total = parts[0] * hits(0, q)
            for j in range(1, KP):
                total = total + parts[j] * hits(j, q)
            tiles.append(total.astype(jnp.bfloat16))
        return tiles

    @pl.loop(0, NB)
    def _(n):
        def hits(j, q):
            return jnp.where(half + 2 * q == pcol[0, n, j], 1.0, 0.0)

        for q, tile in enumerate(placed(p_v[n].astype(jnp.float32), hits)):
            ext[n, :, q * 128:(q + 1) * 128] = tile

    own_t[...] = ext[...].reshape(NB * BS, W).T.reshape(NCOL, 2, BS // 2, NB * BS)

    def spread(n, first, tiles):
        block = a_v[n].astype(jnp.float32)
        parts = []
        for m in range(3):
            parts += doubled(block[:, m * 128:(m + 1) * 128], low)
        last = block[:, 384:448]
        parts.append(jnp.concatenate([last, last], axis=1))
        codes = []
        for k in range(KA):
            code = acol[0, n, k]
            codes.append(code if k < KS else jnp.where(mush[0, n] > 0, code, -1))
        for q in range(first, first + tiles):
            total = parts[0] * jnp.where(half + 2 * q == codes[0], 1.0, 0.0)
            for k in range(1, KA):
                total = total + parts[k] * jnp.where(half + 2 * q == codes[k], 1.0, 0.0)
            high = total.astype(jnp.bfloat16)
            rest = (total - high.astype(jnp.float32)).astype(jnp.bfloat16)
            amat[0, n, :, q * 128:(q + 1) * 128] = high
            amat[1, n, :, q * 128:(q + 1) * 128] = rest

    def product(lo, hi, rows):
        wide = hi - lo
        high = amat[0, :, :, lo:hi].reshape(NB * BS, wide)
        rest = amat[1, :, :, lo:hi].reshape(NB * BS, wide)
        total = jnp.dot(high, rows, preferred_element_type=jnp.float32)
        total = total + jnp.dot(rest, rows, preferred_element_type=jnp.float32)
        return total.astype(jnp.bfloat16)

    def tile_rows(part, ap):
        mine = own_t[:, pl.ds(1 - core, 1)].reshape(NCOL * BS // 2, NB * BS)
        away = jnp.dot(mine, ap, preferred_element_type=jnp.float32)
        psend[part] = away.astype(jnp.bfloat16).reshape(NCOL, BS // 2, W)
        pairs[part].start()
        mine = own_t[:, pl.ds(core, 1)].reshape(NCOL * BS // 2, NB * BS)
        stay = jnp.dot(mine, ap, preferred_element_type=jnp.float32)
        keep[part] = stay.reshape(NCOL, BS // 2, W)

    def summed(part, t):
        return keep[part, t] + precv[part, t].astype(jnp.float32)

    def hop(part, s):
        value = summed(part, chip(4 - s))
        if s > 0:
            chain_a[part][s - 1].wait_recv()
            value = value + cra[part, s - 1].astype(jnp.float32)
        csa[part, s] = value.astype(jnp.bfloat16)
        chain_a[part][s].start()
        if s < 3:
            value = summed(part, chip(s - 3))
            if s > 0:
                chain_b[part][s - 1].wait_recv()
                value = value + crb[part, s - 1].astype(jnp.float32)
            csb[part, s] = value.astype(jnp.bfloat16)
            chain_b[part][s].start()

    def finish(part):
        value = summed(part, yc)
        chain_b[part][2].wait_recv()
        value = value + crb[part, 2].astype(jnp.float32)
        chain_a[part][3].wait_recv()
        value = value + cra[part, 3].astype(jnp.float32)
        out_ref[0, :, part * W:(part + 1) * W] = value

    load_a.wait()

    @pl.loop(0, NB)
    def _(n):
        spread(n, 0, 4)

    tile_rows(OWN, product(0, W, ext[...].reshape(NB * BS, W)))

    @pl.loop(0, NB)
    def _(n):
        spread(n, 4, 4)

    def ghost_product(side):
        ghosts[side].wait_recv()
        there = (gx > 0, gx < nx - 1)[side]
        codes = jnp.where(there, grecv[side, GHOST:GHOST + 16, :128].astype(jnp.float32), -1.0)
        for i in range(G):
            def hits(j, q):
                code = codes[i * KP + j:i * KP + j + 1, :]
                return jnp.where(half_f + 2.0 * q == code, 1.0, 0.0)

            block = grecv[side, i * BS:(i + 1) * BS, :].astype(jnp.float32)
            for q, tile in enumerate(placed(block, hits)):
                gext[side, i * BS:(i + 1) * BS, q * 128:(q + 1) * 128] = tile
        lo = W + side * GHOST
        return product(lo, lo + GHOST, gext[side])

    ap = ghost_product(0)
    pairs[OWN].wait_recv()
    hop(OWN, 0)
    tile_rows(LEFT, ap)
    ap = ghost_product(1)
    hop(OWN, 1)
    tile_rows(RIGHT, ap)
    pairs[LEFT].wait_recv()
    hop(LEFT, 0)
    hop(OWN, 2)
    pairs[RIGHT].wait_recv()
    hop(RIGHT, 0)
    hop(LEFT, 1)
    hop(OWN, 3)
    hop(RIGHT, 1)
    hop(LEFT, 2)
    finish(OWN)
    hop(RIGHT, 2)
    hop(LEFT, 3)
    hop(RIGHT, 3)
    finish(LEFT)
    finish(RIGHT)
    for copy in ghosts + pairs + sum(chain_a, []) + sum(chain_b, []):
        copy.wait_send()


def solution(mesh):
    nx, ny = mesh.shape["gx"], mesh.shape["gy"]

    def body(a_blocks, a_cols, mushy, p_blocks, p_cols, send_rows):
        smem = pl.BlockSpec(memory_space=pltpu.SMEM)
        hbm = pl.BlockSpec(memory_space=pl.ANY)
        bf16, f32 = jnp.bfloat16, jnp.float32
        dma = pltpu.SemaphoreType.DMA
        rows = BS // 2

        def run(*refs):
            kernel(nx, ny, *refs)

        return pl.pallas_call(
            run,
            name="galerkin",
            out_shape=jax.ShapeDtypeStruct((1, rows, 3 * W), f32),
            in_specs=[smem, smem, smem, smem, hbm, hbm],
            out_specs=pl.BlockSpec(memory_space=pltpu.VMEM),
            scratch_shapes=[
                pltpu.VMEM((NB, BS, KA * BS), bf16),
                pltpu.VMEM((NB, BS, KP * BS), bf16),
                pltpu.VMEM((2, GHOST + 16, KP * BS), bf16),
                pltpu.VMEM((2, GHOST + 16, KP * BS), bf16),
                pltpu.VMEM((NB, BS, W), bf16),
                pltpu.VMEM((2, GHOST, W), bf16),
                pltpu.VMEM((2, NB, BS, 2 * NB * BS), bf16),
                pltpu.VMEM((NCOL, 2, rows, NB * BS), bf16),
                pltpu.VMEM((3, NCOL, rows, W), f32),
                pltpu.VMEM((3, NCOL, rows, W), bf16),
                pltpu.VMEM((3, NCOL, rows, W), bf16),
                pltpu.VMEM((3, 4, rows, W), bf16),
                pltpu.VMEM((3, 3, rows, W), bf16),
                pltpu.VMEM((3, 4, rows, W), bf16),
                pltpu.VMEM((3, 3, rows, W), bf16),
                dma((2,)), dma((2,)), dma((2,)), dma((3,)), dma((3,)),
                dma((3, 4)), dma((3, 4)), dma((3, 3)), dma((3, 3)),
            ],
            compiler_params=pltpu.CompilerParams(
                collective_id=0, has_side_effects=True, vmem_limit_bytes=48 * 1024 * 1024),
        )(a_cols, mushy, p_cols, send_rows, a_blocks, p_blocks)

    placed_as = (
        P("gx", "gy", None, None),
        P("gx", "gy", None),
        P("gx", "gy"),
        P("gx", "gy", None, None),
        P("gx", "gy", None),
        P("gx", "gy"),
    )
    return jax.shard_map(
        body, mesh=mesh, in_specs=placed_as, out_specs=P("gx", "gy", None), check_vma=False
    )
```
